32 devices in a mesh: rep: 4 (over y, x), ep: 8 (over z, core).
Axes of the slice: x: 2, y: 2, z: 4, core: 2. Of those that a mesh axis runs over, the one named last changes fastest.
Arguments:
- tokens: bfloat16 [2, 8, 4, 4, 4096], P(None, 'ep', 'rep'), may hold values from -6 to 6
- norm_gain: float32 [4096], replicated, may hold values from 0.5 to 1.5
- expert_ids: int32 [2, 8, 4, 4, 8], P(None, 'ep'), may hold values from 0 to 15, all different within a row; in each aligned block of 16 rows (0 to 15, 16 to 31, ..., all dimensions but the last counted through in order) at most 10 rows name the same one
- route_weights: float32 [2, 8, 4, 4, 8], P(None, 'ep'), may hold values from 0.05 to 1
- w_gate: bfloat16 [16, 1536, 4096], P('ep', 'rep'), may hold values from -0.09375 to 0.09375
- w_up: bfloat16 [16, 1536, 4096], P('ep', 'rep'), may hold values from -0.09375 to 0.09375
- w_down: bfloat16 [16, 1536, 4096], P('ep', 'rep'), may hold values from -0.15625 to 0.15625
Outputs:
- mixed: bfloat16 [2, 8, 4, 4, 4096], P(None, 'ep', 'rep')
The draws below stay inside these ranges and needn't reach their ends.
Inputs may be any that keep to these rules, and one draw needn't show every extreme that they name: `expert_ids`: each row names 8 different experts. In each step, among the rows of one index of ep (16 rows, an aligned block), no expert is named by more than 10 rows, a bound that some block reaches.
All inputs are finite; a program needn't handle non-finite values.
Results may differ from the reference program's by a relative error of at most 0.014.
Values may be sent and summed in bfloat16 or wider, within the bound.
A program may use at most 128 MiB of HBM per device.

```python
import math
import jax
import jax.numpy as jnp
import numpy as np
from jax import lax

D = 4096
F = 1536
TOPK = 8
STEPS = 2
ROWS_DEV = 4
E = 16
FR = 384
TOKENS = 128
CAP = 10
N_REP = 4
N_EP = 8


def levels(own_key, dims, pieces, smallest, high):
    gain, own = 1.0, jax.random.fold_in(own_key, 6)
    for axis_at, parts in pieces:
        steps = jnp.exp(jax.random.uniform(jax.random.fold_in(own, axis_at), (parts,), jnp.float32, smallest / len(pieces), high / len(pieces)))
        gain = gain * jnp.repeat(steps, dims[axis_at] // parts).reshape([-1 if axis == axis_at else 1 for axis in range(len(dims))])
    return gain


def routed_block(stream_key, own, number, rows, number_of, top, limit, lean):
    order = jax.random.permutation(stream_key, number_of)
    packed, usual = load_shares(number_of, rows * top, limit, lean, True), load_shares(number_of, rows * top, limit, lean, False)
    places = jnp.arange(number_of)

    def named(lengths, offset_by):
        used = int((lengths > 0).sum())
        fixed = max(1, used // 4)
        moved = fixed + (places - fixed + offset_by * (used - fixed)) % max(1, number_of - fixed)
        return jnp.zeros((number_of,), jnp.int32).at[order[jnp.where(places < fixed, places, moved)]].set(jnp.asarray(lengths, jnp.int32))

    lengths = jnp.where(number % 4 == 0, named(packed, number // 4), named(usual, number - number // 4 - 1))
    mixed = jax.random.permutation(jax.random.fold_in(own, 3), number_of)
    source_of, taker = mixed[0:number_of // 2 * 2:2], mixed[1:number_of // 2 * 2:2]
    margin = jnp.minimum(lengths[source_of] - 1, limit - lengths[taker]) // 2
    margin = jnp.where((source_of == order[0]) | (taker == order[0]) | (lengths[taker] == 0), 0, jnp.maximum(margin, 0))
    moved = jax.random.randint(jax.random.fold_in(own, 4), (number_of // 2,), 0, 1 << 20) % (margin + 1)
    lengths = lengths.at[source_of].add(-moved).at[taker].add(moved)
    items = jnp.searchsorted(jnp.cumsum(lengths), jnp.arange(rows * top), side="right").astype(jnp.int32)
    listing = items.reshape(top, rows).T
    listing = listing[jax.random.permutation(jax.random.fold_in(own, 1), rows)]
    offset_by = jax.random.randint(jax.random.fold_in(own, 2), (rows, 1), 0, top)
    return jnp.take_along_axis(listing, (jnp.arange(top)[None, :] + offset_by) % top, axis=1)


def load_shares(count, total, limit, skew, full):
    weights = [(1 << 20) // math.isqrt(grade ** skew) + 1 for grade in range(1, count + 1)]
    largest = limit if full else min(limit, max(-(-total // count), total * weights[0] // sum(weights)))
    least = 1 if total - largest >= count - 1 else 0
    given, spare = [largest] + [least] * (count - 1), total - largest - least * (count - 1)
    while spare > 0:
        free = [i for i in range(1, count) if given[i] < largest] or [i for i in range(1, count) if given[i] < limit]
        whole, left = sum([weights[i] for i in free]), spare
        for i in free:
            extra = min(limit - given[i], max(1, left * weights[i] // whole), spare)
            given[i] = given[i] + extra
            spare = spare - extra
    return np.array(given)


def bell_draw(key, dims, spread, limit, split=(), held_as=jnp.bfloat16):
    loudness = levels(key, dims, split, -0.22, 0.18) if split else 1.0
    result = jax.random.normal(key, dims, jnp.float32) * spread * loudness
    return jnp.minimum(jnp.maximum(result, -limit), limit).astype(held_as)


def setup_inputs(seed: int = 0) -> dict:
    streams_of = jax.random.split(jax.random.key(seed), 8)
    tokens = bell_draw(streams_of[0], (STEPS, N_EP, N_REP, ROWS_DEV, D), 1.0, 6.0, ((1, 8), (2, 4)))
    norm_gain = jnp.clip(1.0 + 0.1 * jax.random.normal(streams_of[1], (D,), jnp.float32), 0.5, 1.5)
    expert_ids_keys = jax.random.split(jax.random.fold_in(streams_of[2], 1), STEPS * N_EP * N_REP * ROWS_DEV // (N_REP * ROWS_DEV))
    expert_ids_turns = jax.random.permutation(jax.random.fold_in(streams_of[2], 3), STEPS * N_EP * N_REP * ROWS_DEV // (N_REP * ROWS_DEV))
    expert_ids = jax.vmap(lambda own, number: routed_block(jax.random.fold_in(streams_of[2], 2), own, number, N_REP * ROWS_DEV, E, TOPK, CAP, 2))(expert_ids_keys, expert_ids_turns).reshape((STEPS, N_EP, N_REP, ROWS_DEV, TOPK))
    route_weights = jnp.clip(jnp.exp(math.log(1.0) - 2.9957323 * jax.random.uniform(streams_of[3], (STEPS, N_EP, N_REP, ROWS_DEV, TOPK), jnp.float32) ** levels(streams_of[3], (STEPS, N_EP, N_REP, ROWS_DEV, TOPK), ((1, 8),), -0.2, 0.2)), 0.05, 1.0)
    w_gate = bell_draw(streams_of[4], (E, F, D), D ** -0.5, 0.09375, ((0, 8), (1, 4)))
    w_up = bell_draw(streams_of[5], (E, F, D), D ** -0.5, 0.09375, ((0, 8), (1, 4)))
    w_down = bell_draw(streams_of[6], (E, F, D), F ** -0.5, 0.15625, ((0, 8), (1, 4)))
    return dict(tokens=tokens, norm_gain=norm_gain, expert_ids=expert_ids, route_weights=route_weights, w_gate=w_gate, w_up=w_up, w_down=w_down)


epsilon = 1e-06

def norm_rows(values, gain_values):
    widened = values.astype(jnp.float32)
    scaled = lax.rsqrt(lax.optimization_barrier(jnp.mean(widened * widened, axis=-1, keepdims=True)) + epsilon)
    return (widened * scaled * gain_values).astype(jnp.bfloat16)

def reference(tokens, norm_gain, expert_ids, route_weights, w_gate, w_up, w_down):
    groups = F // FR
    row_limit = N_EP * CAP
    flat_tokens = tokens.reshape(STEPS, TOKENS, D)
    flat_ids = expert_ids.reshape(STEPS, TOKENS, TOPK)
    flat_weights = route_weights.reshape(STEPS, TOKENS, TOPK)
    outputs = []
    for step_index in range(STEPS):
        normed = norm_rows(flat_tokens[step_index], norm_gain)
        step_weights = flat_weights[step_index]
        shares = step_weights / lax.optimization_barrier(jnp.sum(step_weights, axis=-1, keepdims=True))
        chosen_ids = flat_ids[step_index]

        def add_expert(mixed_sum, expert):
            chosen = chosen_ids == expert
            row_weight = lax.optimization_barrier(jnp.sum(jnp.where(chosen, shares, 0.0), axis=-1))
            picked = jnp.any(chosen, axis=-1)
            where_rows = jnp.nonzero(picked, size=row_limit, fill_value=TOKENS)[0].astype(jnp.int32)
            picked_rows = jnp.take(normed, where_rows, axis=0, mode='clip')
            gate_out = jnp.dot(picked_rows, w_gate[expert].T, preferred_element_type=jnp.float32)
            up_out = jnp.dot(picked_rows, w_up[expert].T, preferred_element_type=jnp.float32)
            hidden = (jax.nn.silu(gate_out) * up_out).astype(jnp.bfloat16)
            group_parts = jnp.einsum('mgf,gfd->mgd', hidden.reshape(row_limit, groups, FR).astype(jnp.float32), w_down[expert].reshape(groups, FR, D).astype(jnp.float32))
            rounded = lax.optimization_barrier(group_parts.astype(jnp.bfloat16))
            expert_out = lax.optimization_barrier(jnp.sum(rounded.astype(jnp.float32), axis=1))
            weights_here = jnp.take(row_weight, where_rows, axis=0, mode='clip')
            mixed_sum = mixed_sum.at[where_rows].add(weights_here[:, None] * expert_out, mode='drop')
            return (mixed_sum, None)
        mixed_sum, unused = lax.scan(add_expert, jnp.zeros((TOKENS, D), jnp.float32), jnp.arange(E, dtype=jnp.int32))
        outputs.append(mixed_sum.astype(jnp.bfloat16))
    return jnp.stack(outputs).reshape(STEPS, N_EP, N_REP, ROWS_DEV, D)
```

```python
import jax
import jax.numpy as jnp
from jax import lax
from jax.experimental import pallas as pl
from jax.experimental.pallas import tpu as pltpu
from jax.sharding import PartitionSpec as P

epsilon = 1e-06


def norm_rows(values, gain_values):
    widened = values.astype(jnp.float32)
    scaled = lax.rsqrt(jnp.mean(widened * widened, axis=-1, keepdims=True) + epsilon)
    return (widened * scaled * gain_values).astype(jnp.bfloat16)


def expert_partial(slot_rows, gate_weight, up_weight, down_weight):
    contract_last = (((1,), (1,)), ((), ()))
    gate_out = lax.dot_general(
        slot_rows, gate_weight, contract_last, preferred_element_type=jnp.float32
    )
    up_out = lax.dot_general(
        slot_rows, up_weight, contract_last, preferred_element_type=jnp.float32
    )
    hidden = (jax.nn.silu(gate_out) * up_out).astype(jnp.bfloat16)
    return jnp.dot(hidden, down_weight, preferred_element_type=jnp.float32).astype(jnp.bfloat16)


def weigh_choices(shares, picked):
    choice_total = picked.shape[1]
    weighted = shares[:, 0:1] * picked[:, 0]
    for which in range(1, choice_total):
        weighted = weighted + shares[:, which : which + 1] * picked[:, which]
    return weighted


def routed_on_device(tokens, norm_gain, expert_ids, route_weights, w_gate, w_up, w_down):
    ep_size = lax.axis_size("ep")
    rep_size = lax.axis_size("rep")
    step_count = tokens.shape[0]
    row_count = tokens.shape[3]
    model_width = tokens.shape[4]
    choice_count = expert_ids.shape[4]
    local_experts = w_gate.shape[0]
    experts = local_experts * ep_size
    block_rows = rep_size * row_count
    capacity = block_rows * choice_count * 5 // (4 * experts)
    column_width = model_width // rep_size
    assigned = block_rows * choice_count
    row_of = jnp.arange(assigned, dtype=jnp.int32) // choice_count
    outputs = []
    for step_index in range(step_count):
        own_normed = norm_rows(tokens[step_index, 0, 0], norm_gain)
        step_weights = route_weights[step_index].reshape(block_rows, choice_count)
        shares = step_weights / jnp.sum(step_weights, axis=1, keepdims=True)
        chosen_ids = expert_ids[step_index].reshape(assigned)
        target = chosen_ids // local_experts
        slot_index = chosen_ids % local_experts
        buckets = ep_size * local_experts
        bucket = target * local_experts + slot_index
        onehot = (bucket[:, None] == jnp.arange(buckets, dtype=jnp.int32)[None, :]).astype(
            jnp.int32
        )
        position = jnp.sum((jnp.cumsum(onehot, axis=0) - onehot) * onehot, axis=1)
        flat_index = bucket * capacity + position
        source_row = (
            jnp.full((buckets * capacity,), block_rows, jnp.int32).at[flat_index].set(row_of)
        )
        own_part = lax.all_to_all(own_normed, "rep", split_axis=1, concat_axis=0, tiled=True)
        padded = jnp.concatenate([own_part, jnp.zeros((1, column_width), jnp.bfloat16)], axis=0)
        outgoing = jnp.take(padded, source_row, axis=0).reshape(
            ep_size, local_experts, capacity, column_width
        )
        received = lax.all_to_all(outgoing, "ep", split_axis=0, concat_axis=0, tiled=True)
        arrived = lax.all_gather(received, "rep", axis=3, tiled=True)
        slot_results = []
        for local_slot in range(local_experts):
            weights_now = (w_gate[local_slot], w_up[local_slot], w_down[local_slot])
            slot_rows = arrived[:, local_slot].reshape(ep_size * capacity, model_width)
            slot_out = expert_partial(slot_rows, weights_now[0], weights_now[1], weights_now[2])
            slot_results.append(slot_out.reshape(ep_size, capacity, model_width))
        results_out = jnp.stack(slot_results, axis=1)
        summed = lax.psum_scatter(
            results_out.astype(jnp.float32).astype(jnp.bfloat16),
            "rep",
            scatter_dimension=3,
            tiled=True,
        ).astype(jnp.float32)
        back = lax.all_to_all(
            summed.astype(jnp.bfloat16), "ep", split_axis=0, concat_axis=0, tiled=True
        ).astype(summed.dtype)
        picked = jnp.take(back.reshape(buckets * capacity, column_width), flat_index, axis=0)
        picked = picked.reshape(block_rows, choice_count, column_width)
        weighted = weigh_choices(shares, picked)
        mixed = (
            lax.all_to_all(
                weighted.astype(jnp.bfloat16), "rep", split_axis=0, concat_axis=1, tiled=True
            )
            .astype(weighted.dtype)
            .astype(jnp.bfloat16)
        )
        outputs.append(mixed)
    return jnp.stack(outputs)[:, None, None]


LANES = 128
HALF = LANES // 2
CHUNKS = 4


def fused_kernel(
    tok_ref, gain_ref, ids_ref, rw_ref, gate_hbm, up_hbm, down_hbm, out_ref,
    wgu, wdn, xg, wx, xs, acc, hs, nrm, wst,
    pbuf, rb0, sb1, rb1, sb2, rb2, sb3, sv, rb3, ost,
    wsem, ag_send, ag_recv, rs_send, rs_recv,
):
    f32, bf16 = jnp.float32, jnp.bfloat16
    steps, rows, width = tok_ref.shape
    nz = xg.shape[4]
    cw = xg.shape[6]
    own_rows = steps * rows
    local_experts, hidden_units = gate_hbm.shape[0], gate_hbm.shape[1]
    choices = ids_ref.shape[3]
    total = 8 * nz * own_rows
    rep, ep = lax.axis_index("rep"), lax.axis_index("ep")
    y, x = rep // 2, rep % 2
    z, core = ep // 2, ep % 2
    partner = (rep, z * 2 + 1 - core)
    over_x = (y * 2 + 1 - x, ep)
    over_y = ((1 - y) * 2 + x, ep)
    along_z = [(rep, ((z + d) % nz) * 2 + core) for d in range(1, nz)]

    barrier = pltpu.get_barrier_semaphore()
    everyone = [partner, over_x, over_y] + along_z
    for device in everyone:
        pl.semaphore_signal(barrier, inc=1, device_id=device, device_id_type=pl.DeviceIdType.MESH)

    loads = []
    for j in range(local_experts):
        loads.append(pltpu.make_async_copy(gate_hbm.at[j], wgu.at[j], wsem.at[len(loads)]))
        loads.append(pltpu.make_async_copy(up_hbm.at[j], wgu.at[local_experts + j], wsem.at[len(loads)]))
    downs = []
    for j in range(local_experts):
        downs.append(
            pltpu.make_async_copy(
                down_hbm.at[j],
                wdn.at[pl.ds(j * hidden_units, hidden_units)],
                wsem.at[len(loads) + j],
            )
        )
    for load in loads + downs:
        load.start()

    lane = lax.broadcasted_iota(jnp.int32, (rows, LANES), 1)
    for s in range(steps):
        nrm[pl.ds(s * rows, rows), :] = tok_ref[s].astype(f32)
        weights_now = rw_ref[s, rep]
        ids_now = ids_ref[s, rep]
        shares = weights_now / jnp.sum(weights_now, axis=1, keepdims=True)
        dense = jnp.zeros((rows, LANES), f32)
        for k in range(choices):
            dense = dense + jnp.where((lane & (HALF - 1)) == ids_now[:, k : k + 1], shares[:, k : k + 1], 0.0)
        wst[pl.ds(s * rows, rows), :] = dense
    dense = wst[...]
    high = dense.astype(bf16).astype(f32)
    wide_lane = lax.broadcasted_iota(jnp.int32, (own_rows, LANES), 1)
    wx[core, y, x, z] = jnp.where(wide_lane < HALF, high, dense - high).astype(bf16)
    values = nrm[...]
    scaled = lax.rsqrt(jnp.mean(values * values, axis=-1, keepdims=True) + epsilon)
    for c in range(CHUNKS):
        cols = pl.ds(c * cw, cw)
        xg[c, core, y, x, z] = (nrm[:, cols] * scaled * gain_ref[:, cols]).astype(bf16)
    pl.semaphore_wait(barrier, len(everyone))

    started = []

    def send(src, dst, send_sem, recv_sem, device):
        copy = pltpu.make_async_remote_copy(
            src_ref=src, dst_ref=dst, send_sem=send_sem, recv_sem=recv_sem,
            device_id=device, device_id_type=pl.DeviceIdType.MESH,
        )
        copy.start()
        started.append(copy)
        return copy

    bufs = [xg.at[c] for c in range(CHUNKS)] + [wx]
    order = [CHUNKS] + list(range(CHUNKS))
    x_first = [c % 2 == 0 for c in range(CHUNKS)] + [False]
    first_device = [over_x if flag else over_y for flag in x_first]
    second_device = [over_y if flag else over_x for flag in x_first]

    hop_z, hop_1, hop_2, share_1, share_2, share_3 = {}, {}, {}, {}, {}, {}

    def ag_send_to(c, slot, where, device):
        ref = bufs[c].at[where]
        return send(ref, ref, ag_send.at[c, slot], ag_recv.at[c, slot], device)

    for c in order:
        hop_z[c] = [ag_send_to(c, d, (core, y, x, z), along_z[d]) for d in range(nz - 1)]
    for c in order:
        for copy in hop_z[c]:
            copy.wait_recv()
        hop_1[c] = ag_send_to(c, nz - 1, (core, y, x), first_device[c])
        share_1[c] = ag_send_to(c, nz + 1, (core, y, x), partner)
    for c in order:
        hop_1[c].wait_recv()
        if x_first[c]:
            hop_2[c] = ag_send_to(c, nz, (core, y), second_device[c])
            share_2[c] = ag_send_to(c, nz + 2, (core, y, 1 - x), partner)
        else:
            hop_2[c] = ag_send_to(c, nz, (core, slice(None), x), second_device[c])
            share_2[c] = ag_send_to(c, nz + 2, (core, 1 - y, x), partner)

    def finish_gather(c):
        hop_2[c].wait_recv()
        where = (core, 1 - y) if x_first[c] else (core, slice(None), 1 - x)
        share_3[c] = ag_send_to(c, nz + 3, where, partner)

    def arrived(c):
        for copy in (share_1[c], share_2[c], share_3[c]):
            copy.wait_recv()

    def gate_up(c):
        arrived(c)
        xs[...] = xg[c].astype(f32).reshape(total, cw).astype(bf16)
        if c == 0:
            for load in loads:
                load.wait()

        def one(i, carry):
            part = lax.dot_general(
                xs[...], wgu[i, :, pl.ds(c * cw, cw)],
                (((1,), (1,)), ((), ())), preferred_element_type=f32,
            )
            acc[i] = part if c == 0 else acc[i] + part
            return carry

        lax.fori_loop(0, 2 * local_experts, one, 0)

    for at, c in enumerate(order):
        finish_gather(c)
        if at >= 2:
            gate_up(order[at - 1])
    gate_up(order[-1])
    arrived(CHUNKS)

    row_weights = wx[...].astype(f32).reshape(total, LANES)
    all_lane = lax.broadcasted_iota(jnp.int32, (total, LANES), 1) & (HALF - 1)
    for j in range(local_experts):
        mine = jnp.sum(
            jnp.where(all_lane == ep * local_experts + j, row_weights, 0.0), axis=1, keepdims=True
        )
        gate_out, up_out = acc[j], acc[local_experts + j]
        hs[:, pl.ds(j * hidden_units, hidden_units)] = (jax.nn.silu(gate_out) * up_out * mine).astype(bf16)
    for load in downs:
        load.wait()

    to_core, to_first, to_second, to_z = {}, {}, {}, {}

    def rs_send_to(c, slot, src, dst, device):
        return send(src, dst, rs_send.at[c, slot], rs_recv.at[c, slot], device)

    def place(c, first, second):
        return (second, first) if x_first[c] else (first, second)

    me_first = [x if x_first[c] else y for c in range(CHUNKS)]
    me_second = [y if x_first[c] else x for c in range(CHUNKS)]

    def pair_sum(c, first, second):
        where = place(c, first, second)
        return pbuf[(c, core) + where].astype(f32) + rb0[(c,) + where].astype(f32)

    def down(c):
        half = cw // 2
        for piece in range(2):
            part = jnp.dot(
                hs[...], wdn[:, pl.ds(c * cw + piece * half, half)], preferred_element_type=f32
            )
            pbuf[c, :, :, :, :, :, pl.ds(piece * half, half)] = part.reshape(
                2, 2, 2, nz, own_rows, half
            ).astype(bf16)
        to_core[c] = rs_send_to(c, nz - 1, pbuf.at[c, 1 - core], rb0.at[c], partner)

    def stage_1(c):
        to_core[c].wait_recv()
        for second in range(2):
            sb1[c, second] = pair_sum(c, 1 - me_first[c], second).astype(bf16)
        to_first[c] = rs_send_to(c, nz, sb1.at[c], rb1.at[c], first_device[c])

    def stage_2(c):
        to_first[c].wait_recv()
        other = 1 - me_second[c]
        sb2[c] = (pair_sum(c, me_first[c], other) + rb1[c, other].astype(f32)).astype(bf16)
        to_second[c] = rs_send_to(c, nz + 1, sb2.at[c], rb2.at[c], second_device[c])

    def stage_3(c):
        to_second[c].wait_recv()
        mine = pair_sum(c, me_first[c], me_second[c]) + rb1[c, me_second[c]].astype(f32) + rb2[c].astype(f32)
        sv[c] = mine
        sb3[c] = mine.astype(bf16)
        to_z[c] = [
            rs_send_to(c, d, sb3.at[c, (z + d + 1) % nz], rb3.at[c, d], along_z[d])
            for d in range(nz - 1)
        ]

    def finish(c):
        whole = sv[c, z]
        for d in range(nz - 1):
            to_z[c][d].wait_recv()
            whole = whole + rb3[c, d].astype(f32)
        ost[:, pl.ds(c * cw, cw)] = whole

    for c in range(CHUNKS):
        down(c)
        if c >= 1:
            stage_1(c - 1)
    stage_1(CHUNKS - 1)
    for c in range(CHUNKS):
        stage_2(c)
    for c in range(CHUNKS):
        stage_3(c)
    for c in range(CHUNKS):
        finish(c)
    for s in range(steps):
        out_ref[s] = ost[pl.ds(s * rows, rows), :].astype(bf16)
    for copy in started:
        copy.wait_send()


def fused_on_device(tokens, norm_gain, expert_ids, route_weights, w_gate, w_up, w_down):
    steps, rows, width = tokens.shape[0], tokens.shape[3], tokens.shape[4]
    nz = lax.axis_size("ep") // 2
    local_experts, hidden_units = w_gate.shape[0], w_gate.shape[1]
    own_rows = steps * rows
    cw = width // CHUNKS
    total = 8 * nz * own_rows
    f32, bf16 = jnp.float32, jnp.bfloat16
    vmem = pl.BlockSpec(memory_space=pltpu.VMEM)
    hbm = pl.BlockSpec(memory_space=pl.ANY)
    grid_rows = (nz, own_rows, cw)
    out = pl.pallas_call(
        fused_kernel,
        out_shape=jax.ShapeDtypeStruct((steps, rows, width), bf16),
        in_specs=[vmem] * 4 + [hbm] * 3,
        out_specs=vmem,
        scratch_shapes=[
            pltpu.VMEM((2 * local_experts, hidden_units, width), bf16),
            pltpu.VMEM((local_experts * hidden_units, width), bf16),
            pltpu.VMEM((CHUNKS, 2, 2, 2) + grid_rows, bf16),
            pltpu.VMEM((2, 2, 2, nz, own_rows, LANES), bf16),
            pltpu.VMEM((total, cw), bf16),
            pltpu.VMEM((2 * local_experts, total, hidden_units), f32),
            pltpu.VMEM((total, local_experts * hidden_units), bf16),
            pltpu.VMEM((own_rows, width), f32),
            pltpu.VMEM((own_rows, LANES), f32),
            pltpu.VMEM((CHUNKS, 2, 2, 2) + grid_rows, bf16),
            pltpu.VMEM((CHUNKS, 2, 2) + grid_rows, bf16),
            pltpu.VMEM((CHUNKS, 2) + grid_rows, bf16),
            pltpu.VMEM((CHUNKS, 2) + grid_rows, bf16),
            pltpu.VMEM((CHUNKS,) + grid_rows, bf16),
            pltpu.VMEM((CHUNKS,) + grid_rows, bf16),
            pltpu.VMEM((CHUNKS,) + grid_rows, bf16),
            pltpu.VMEM((CHUNKS,) + grid_rows, f32),
            pltpu.VMEM((CHUNKS, nz - 1, own_rows, cw), bf16),
            pltpu.VMEM((own_rows, width), f32),
            pltpu.SemaphoreType.DMA((3 * local_experts,)),
            pltpu.SemaphoreType.DMA((CHUNKS + 1, nz + 4)),
            pltpu.SemaphoreType.DMA((CHUNKS + 1, nz + 4)),
            pltpu.SemaphoreType.DMA((CHUNKS, nz + 2)),
            pltpu.SemaphoreType.DMA((CHUNKS, nz + 2)),
        ],
        compiler_params=pltpu.CompilerParams(
            collective_id=0, has_side_effects=True, vmem_limit_bytes=60 * 1024 * 1024
        ),
    )(
        tokens[:, 0, 0],
        norm_gain[None, :],
        expert_ids[:, 0],
        route_weights[:, 0],
        w_gate,
        w_up,
        w_down,
    )
    return out[:, None, None]


def on_device(tokens, norm_gain, expert_ids, route_weights, w_gate, w_up, w_down):
    ep_size, rep_size = lax.axis_size("ep"), lax.axis_size("rep")
    own_rows = tokens.shape[0] * tokens.shape[3]
    experts = w_gate.shape[0] * ep_size
    dense = (
        rep_size == 4
        and ep_size % 2 == 0
        and own_rows == 8
        and experts <= min(HALF, 4 * expert_ids.shape[4])
        and own_rows * rep_size * ep_size <= 512
        and tokens.shape[4] % (2 * CHUNKS * LANES) == 0
        and w_gate.shape[1] % LANES == 0
    )
    run = fused_on_device if dense else routed_on_device
    return run(tokens, norm_gain, expert_ids, route_weights, w_gate, w_up, w_down)


def solution(mesh):
    return jax.shard_map(
        on_device,
        mesh=mesh,
        in_specs=(
            P(None, "ep", "rep", None, None),
            P(),
            P(None, "ep", None, None, None),
            P(None, "ep", None, None, None),
            P("ep", "rep", None),
            P("ep", "rep", None),
            P("ep", "rep", None),
        ),
        out_specs=P(None, "ep", "rep", None, None),
        check_vma=False,
    )
```

```python
import jax
import jax.numpy as jnp
from jax import lax
from jax.experimental import pallas as pl
from jax.experimental.pallas import tpu as pltpu
from jax.sharding import PartitionSpec as P

epsilon = 1e-06


def norm_rows(values, gain_values):
    widened = values.astype(jnp.float32)
    scaled = lax.rsqrt(jnp.mean(widened * widened, axis=-1, keepdims=True) + epsilon)
    return (widened * scaled * gain_values).astype(jnp.bfloat16)


def expert_partial(slot_rows, gate_weight, up_weight, down_weight):
    contract_last = (((1,), (1,)), ((), ()))
    gate_out = lax.dot_general(
        slot_rows, gate_weight, contract_last, preferred_element_type=jnp.float32
    )
    up_out = lax.dot_general(
        slot_rows, up_weight, contract_last, preferred_element_type=jnp.float32
    )
    hidden = (jax.nn.silu(gate_out) * up_out).astype(jnp.bfloat16)
    return jnp.dot(hidden, down_weight, preferred_element_type=jnp.float32).astype(jnp.bfloat16)


def weigh_choices(shares, picked):
    choice_total = picked.shape[1]
    weighted = shares[:, 0:1] * picked[:, 0]
    for which in range(1, choice_total):
        weighted = weighted + shares[:, which : which + 1] * picked[:, which]
    return weighted


def routed_on_device(tokens, norm_gain, expert_ids, route_weights, w_gate, w_up, w_down):
    ep_size = lax.axis_size("ep")
    rep_size = lax.axis_size("rep")
    step_count = tokens.shape[0]
    row_count = tokens.shape[3]
    model_width = tokens.shape[4]
    choice_count = expert_ids.shape[4]
    local_experts = w_gate.shape[0]
    experts = local_experts * ep_size
    block_rows = rep_size * row_count
    capacity = block_rows * choice_count * 5 // (4 * experts)
    column_width = model_width // rep_size
    assigned = block_rows * choice_count
    row_of = jnp.arange(assigned, dtype=jnp.int32) // choice_count
    outputs = []
    for step_index in range(step_count):
        own_normed = norm_rows(tokens[step_index, 0, 0], norm_gain)
        step_weights = route_weights[step_index].reshape(block_rows, choice_count)
        shares = step_weights / jnp.sum(step_weights, axis=1, keepdims=True)
        chosen_ids = expert_ids[step_index].reshape(assigned)
        target = chosen_ids // local_experts
        slot_index = chosen_ids % local_experts
        buckets = ep_size * local_experts
        bucket = target * local_experts + slot_index
        onehot = (bucket[:, None] == jnp.arange(buckets, dtype=jnp.int32)[None, :]).astype(
            jnp.int32
        )
        position = jnp.sum((jnp.cumsum(onehot, axis=0) - onehot) * onehot, axis=1)
        flat_index = bucket * capacity + position
        source_row = (
            jnp.full((buckets * capacity,), block_rows, jnp.int32).at[flat_index].set(row_of)
        )
        own_part = lax.all_to_all(own_normed, "rep", split_axis=1, concat_axis=0, tiled=True)
        padded = jnp.concatenate([own_part, jnp.zeros((1, column_width), jnp.bfloat16)], axis=0)
        outgoing = jnp.take(padded, source_row, axis=0).reshape(
            ep_size, local_experts, capacity, column_width
        )
        received = lax.all_to_all(outgoing, "ep", split_axis=0, concat_axis=0, tiled=True)
        arrived = lax.all_gather(received, "rep", axis=3, tiled=True)
        slot_results = []
        for local_slot in range(local_experts):
            weights_now = (w_gate[local_slot], w_up[local_slot], w_down[local_slot])
            slot_rows = arrived[:, local_slot].reshape(ep_size * capacity, model_width)
            slot_out = expert_partial(slot_rows, weights_now[0], weights_now[1], weights_now[2])
            slot_results.append(slot_out.reshape(ep_size, capacity, model_width))
        results_out = jnp.stack(slot_results, axis=1)
        summed = lax.psum_scatter(
            results_out.astype(jnp.float32).astype(jnp.bfloat16),
            "rep",
            scatter_dimension=3,
            tiled=True,
        ).astype(jnp.float32)
        back = lax.all_to_all(
            summed.astype(jnp.bfloat16), "ep", split_axis=0, concat_axis=0, tiled=True
        ).astype(summed.dtype)
        picked = jnp.take(back.reshape(buckets * capacity, column_width), flat_index, axis=0)
        picked = picked.reshape(block_rows, choice_count, column_width)
        weighted = weigh_choices(shares, picked)
        mixed = (
            lax.all_to_all(
                weighted.astype(jnp.bfloat16), "rep", split_axis=0, concat_axis=1, tiled=True
            )
            .astype(weighted.dtype)
            .astype(jnp.bfloat16)
        )
        outputs.append(mixed)
    return jnp.stack(outputs)[:, None, None]


LANES = 128
HALF = LANES // 2
CHUNKS = 4


def fused_kernel(
    tok_ref, gain_ref, ids_ref, rw_ref, gate_hbm, up_hbm, down_hbm, out_ref,
    wgu, wdn, xg, wx, xs, acc, hs, nrm, wst,
    pbuf, rb0, sb1, rb1, sb2, rb2, sb3, sv, rb3, ost,
    wsem, ag_send, ag_recv, rs_send, rs_recv,
):
    f32, bf16 = jnp.float32, jnp.bfloat16
    steps, rows, width = tok_ref.shape
    nz = xg.shape[4]
    cw = xg.shape[6]
    own_rows = steps * rows
    local_experts, hidden_units = gate_hbm.shape[0], gate_hbm.shape[1]
    choices = ids_ref.shape[3]
    total = 8 * nz * own_rows
    rep, ep = lax.axis_index("rep"), lax.axis_index("ep")
    y, x = rep // 2, rep % 2
    z, core = ep // 2, ep % 2
    partner = (rep, z * 2 + 1 - core)
    over_x = (y * 2 + 1 - x, ep)
    over_y = ((1 - y) * 2 + x, ep)
    along_z = [(rep, ((z + d) % nz) * 2 + core) for d in range(1, nz)]

    barrier = pltpu.get_barrier_semaphore()
    everyone = [partner, over_x, over_y] + along_z
    for device in everyone:
        pl.semaphore_signal(barrier, inc=1, device_id=device, device_id_type=pl.DeviceIdType.MESH)

    loads = []
    for j in range(local_experts):
        loads.append(pltpu.make_async_copy(gate_hbm.at[j], wgu.at[j], wsem.at[len(loads)]))
        loads.append(pltpu.make_async_copy(up_hbm.at[j], wgu.at[local_experts + j], wsem.at[len(loads)]))
    downs = []
    for j in range(local_experts):
        downs.append(
            pltpu.make_async_copy(
                down_hbm.at[j],
                wdn.at[pl.ds(j * hidden_units, hidden_units)],
                wsem.at[len(loads) + j],
            )
        )
    for load in loads + downs:
        load.start()

    for s in range(steps):
        nrm[pl.ds(s * rows, rows), :] = tok_ref[s].astype(f32)
    values = nrm[...]
    scaled = lax.rsqrt(jnp.mean(values * values, axis=-1, keepdims=True) + epsilon)
    for c in range(CHUNKS):
        cols = pl.ds(c * cw, cw)
        xg[c, core, y, x, z] = (nrm[:, cols] * scaled * gain_ref[:, cols]).astype(bf16)
    pl.semaphore_wait(barrier, len(everyone))

    started = []

    def send(src, dst, send_sem, recv_sem, device):
        copy = pltpu.make_async_remote_copy(
            src_ref=src, dst_ref=dst, send_sem=send_sem, recv_sem=recv_sem,
            device_id=device, device_id_type=pl.DeviceIdType.MESH,
        )
        copy.start()
        started.append(copy)
        return copy

    bufs = [xg.at[c] for c in range(CHUNKS)] + [wx]
    order = list(range(CHUNKS)) + [CHUNKS]
    x_first = [c % 2 == 0 for c in range(CHUNKS)] + [False]
    first_device = [over_x if flag else over_y for flag in x_first]
    second_device = [over_y if flag else over_x for flag in x_first]

    hop_z, hop_1, hop_2, share_1, share_2, share_3 = {}, {}, {}, {}, {}, {}

    def ag_send_to(c, slot, where, device):
        ref = bufs[c].at[where]
        return send(ref, ref, ag_send.at[c, slot], ag_recv.at[c, slot], device)

    def hop_along_z(c):
        hop_z[c] = [ag_send_to(c, d, (core, y, x, z), along_z[d]) for d in range(nz - 1)]

    for c in order[:-1]:
        hop_along_z(c)
    lane = lax.broadcasted_iota(jnp.int32, (rows, LANES), 1)
    for s in range(steps):
        weights_now = rw_ref[s, rep]
        ids_now = ids_ref[s, rep]
        shares = weights_now / jnp.sum(weights_now, axis=1, keepdims=True)
        dense = jnp.zeros((rows, LANES), f32)
        for k in range(choices):
            dense = dense + jnp.where((lane & (HALF - 1)) == ids_now[:, k : k + 1], shares[:, k : k + 1], 0.0)
        wst[pl.ds(s * rows, rows), :] = dense
    dense = wst[...]
    high = dense.astype(bf16).astype(f32)
    wide_lane = lax.broadcasted_iota(jnp.int32, (own_rows, LANES), 1)
    wx[core, y, x, z] = jnp.where(wide_lane < HALF, high, dense - high).astype(bf16)
    hop_along_z(CHUNKS)
    for c in order:
        for copy in hop_z[c]:
            copy.wait_recv()
        hop_1[c] = ag_send_to(c, nz - 1, (core, y, x), first_device[c])
        share_1[c] = ag_send_to(c, nz + 1, (core, y, x), partner)
    for c in order:
        hop_1[c].wait_recv()
        if x_first[c]:
            hop_2[c] = ag_send_to(c, nz, (core, y), second_device[c])
            share_2[c] = ag_send_to(c, nz + 2, (core, y, 1 - x), partner)
        else:
            hop_2[c] = ag_send_to(c, nz, (core, slice(None), x), second_device[c])
            share_2[c] = ag_send_to(c, nz + 2, (core, 1 - y, x), partner)

    def finish_gather(c):
        hop_2[c].wait_recv()
        where = (core, 1 - y) if x_first[c] else (core, slice(None), 1 - x)
        share_3[c] = ag_send_to(c, nz + 3, where, partner)

    def arrived(c):
        for copy in (share_1[c], share_2[c], share_3[c]):
            copy.wait_recv()

    def gate_up(c):
        arrived(c)
        xs[...] = xg[c].astype(f32).reshape(total, cw).astype(bf16).T
        if c == 0:
            for load in loads:
                load.wait()

        def one(i, carry):
            part = jnp.dot(wgu[i, :, pl.ds(c * cw, cw)], xs[...], preferred_element_type=f32)
            acc[i] = part if c == 0 else acc[i] + part
            return carry

        lax.fori_loop(0, 2 * local_experts, one, 0)

    for at, c in enumerate(order):
        finish_gather(c)
        if at >= 1:
            gate_up(order[at - 1])
    arrived(CHUNKS)

    row_weights = wx[...].astype(f32).reshape(total, LANES).T
    all_lane = lax.broadcasted_iota(jnp.int32, (LANES, total), 0) & (HALF - 1)
    for j in range(local_experts):
        mine = jnp.sum(
            jnp.where(all_lane == ep * local_experts + j, row_weights, 0.0), axis=0, keepdims=True
        )
        gate_out, up_out = acc[j], acc[local_experts + j]
        hs[:, pl.ds(j * hidden_units, hidden_units)] = (
            jax.nn.silu(gate_out) * up_out * mine
        ).T.astype(bf16)
    for load in downs:
        load.wait()

    to_core, to_first, to_second, to_z = {}, {}, {}, {}

    def rs_send_to(c, slot, src, dst, device):
        return send(src, dst, rs_send.at[c, slot], rs_recv.at[c, slot], device)

    def place(c, first, second):
        return (second, first) if x_first[c] else (first, second)

    me_first = [x if x_first[c] else y for c in range(CHUNKS)]
    me_second = [y if x_first[c] else x for c in range(CHUNKS)]

    def pair_sum(c, first, second):
        where = place(c, first, second)
        return pbuf[(c, core) + where].astype(f32) + rb0[(c,) + where].astype(f32)

    def down(c):
        half = cw // 2
        for piece in range(2):
            part = jnp.dot(
                hs[...], wdn[:, pl.ds(c * cw + piece * half, half)], preferred_element_type=f32
            )
            pbuf[c, :, :, :, :, :, pl.ds(piece * half, half)] = part.reshape(
                2, 2, 2, nz, own_rows, half
            ).astype(bf16)
        to_core[c] = rs_send_to(c, nz - 1, pbuf.at[c, 1 - core], rb0.at[c], partner)

    def stage_1(c):
        to_core[c].wait_recv()
        for second in range(2):
            sb1[c, second] = pair_sum(c, 1 - me_first[c], second).astype(bf16)
        to_first[c] = rs_send_to(c, nz, sb1.at[c], rb1.at[c], first_device[c])

    def stage_2(c):
        to_first[c].wait_recv()
        other = 1 - me_second[c]
        sb2[c] = (pair_sum(c, me_first[c], other) + rb1[c, other].astype(f32)).astype(bf16)
        to_second[c] = rs_send_to(c, nz + 1, sb2.at[c], rb2.at[c], second_device[c])

    def stage_3(c):
        to_second[c].wait_recv()
        mine = pair_sum(c, me_first[c], me_second[c]) + rb1[c, me_second[c]].astype(f32) + rb2[c].astype(f32)
        sv[c] = mine
        sb3[c] = mine.astype(bf16)
        to_z[c] = [
            rs_send_to(c, d, sb3.at[c, (z + d + 1) % nz], rb3.at[c, d], along_z[d])
            for d in range(nz - 1)
        ]

    def finish(c):
        whole = sv[c, z]
        for d in range(nz - 1):
            to_z[c][d].wait_recv()
            whole = whole + rb3[c, d].astype(f32)
        ost[:, pl.ds(c * cw, cw)] = whole

    for c in range(CHUNKS):
        down(c)
        if c >= 1:
            stage_1(c - 1)
    stage_1(CHUNKS - 1)
    for c in range(CHUNKS):
        stage_2(c)
    for c in range(CHUNKS):
        stage_3(c)
    for c in range(CHUNKS):
        finish(c)
    for s in range(steps):
        out_ref[s] = ost[pl.ds(s * rows, rows), :]
    for copy in started:
        copy.wait_send()


def fused_on_device(tokens, norm_gain, expert_ids, route_weights, w_gate, w_up, w_down):
    steps, rows, width = tokens.shape[0], tokens.shape[3], tokens.shape[4]
    nz = lax.axis_size("ep") // 2
    local_experts, hidden_units = w_gate.shape[0], w_gate.shape[1]
    own_rows = steps * rows
    cw = width // CHUNKS
    total = 8 * nz * own_rows
    f32, bf16 = jnp.float32, jnp.bfloat16
    vmem = pl.BlockSpec(memory_space=pltpu.VMEM)
    hbm = pl.BlockSpec(memory_space=pl.ANY)
    grid_rows = (nz, own_rows, cw)
    out = pl.pallas_call(
        fused_kernel,
        out_shape=jax.ShapeDtypeStruct((steps, rows, width), f32),
        in_specs=[vmem] * 4 + [hbm] * 3,
        out_specs=vmem,
        scratch_shapes=[
            pltpu.VMEM((2 * local_experts, hidden_units, width), bf16),
            pltpu.VMEM((local_experts * hidden_units, width), bf16),
            pltpu.VMEM((CHUNKS, 2, 2, 2) + grid_rows, bf16),
            pltpu.VMEM((2, 2, 2, nz, own_rows, LANES), bf16),
            pltpu.VMEM((cw, total), bf16),
            pltpu.VMEM((2 * local_experts, hidden_units, total), f32),
            pltpu.VMEM((total, local_experts * hidden_units), bf16),
            pltpu.VMEM((own_rows, width), f32),
            pltpu.VMEM((own_rows, LANES), f32),
            pltpu.VMEM((CHUNKS, 2, 2, 2) + grid_rows, bf16),
            pltpu.VMEM((CHUNKS, 2, 2) + grid_rows, bf16),
            pltpu.VMEM((CHUNKS, 2) + grid_rows, bf16),
            pltpu.VMEM((CHUNKS, 2) + grid_rows, bf16),
            pltpu.VMEM((CHUNKS,) + grid_rows, bf16),
            pltpu.VMEM((CHUNKS,) + grid_rows, bf16),
            pltpu.VMEM((CHUNKS,) + grid_rows, bf16),
            pltpu.VMEM((CHUNKS,) + grid_rows, f32),
            pltpu.VMEM((CHUNKS, nz - 1, own_rows, cw), bf16),
            pltpu.VMEM((own_rows, width), f32),
            pltpu.SemaphoreType.DMA((3 * local_experts,)),
            pltpu.SemaphoreType.DMA((CHUNKS + 1, nz + 4)),
            pltpu.SemaphoreType.DMA((CHUNKS + 1, nz + 4)),
            pltpu.SemaphoreType.DMA((CHUNKS, nz + 2)),
            pltpu.SemaphoreType.DMA((CHUNKS, nz + 2)),
        ],
        compiler_params=pltpu.CompilerParams(
            collective_id=0, has_side_effects=True, vmem_limit_bytes=60 * 1024 * 1024
        ),
    )(
        tokens[:, 0, 0],
        norm_gain[None, :],
        expert_ids[:, 0],
        route_weights[:, 0],
        w_gate,
        w_up,
        w_down,
    )
    return out.astype(bf16)[:, None, None]


def on_device(tokens, norm_gain, expert_ids, route_weights, w_gate, w_up, w_down):
    ep_size, rep_size = lax.axis_size("ep"), lax.axis_size("rep")
    own_rows = tokens.shape[0] * tokens.shape[3]
    experts = w_gate.shape[0] * ep_size
    dense = (
        rep_size == 4
        and ep_size % 2 == 0
        and own_rows == 8
        and experts <= min(HALF, 4 * expert_ids.shape[4])
        and own_rows * rep_size * ep_size <= 512
        and tokens.shape[4] % (2 * CHUNKS * LANES) == 0
        and w_gate.shape[1] % LANES == 0
    )
    run = fused_on_device if dense else routed_on_device
    return run(tokens, norm_gain, expert_ids, route_weights, w_gate, w_up, w_down)


def solution(mesh):
    return jax.shard_map(
        on_device,
        mesh=mesh,
        in_specs=(
            P(None, "ep", "rep", None, None),
            P(),
            P(None, "ep", None, None, None),
            P(None, "ep", None, None, None),
            P("ep", "rep", None),
            P("ep", "rep", None),
            P("ep", "rep", None),
        ),
        out_specs=P(None, "ep", "rep", None, None),
        check_vma=False,
    )
```

```python
import jax
import jax.numpy as jnp
from jax import lax
from jax.experimental import pallas as pl
from jax.experimental.pallas import tpu as pltpu
from jax.sharding import PartitionSpec as P

epsilon = 1e-06


def norm_rows(values, gain_values):
    widened = values.astype(jnp.float32)
    scaled = lax.rsqrt(jnp.mean(widened * widened, axis=-1, keepdims=True) + epsilon)
    return (widened * scaled * gain_values).astype(jnp.bfloat16)


def expert_partial(slot_rows, gate_weight, up_weight, down_weight):
    contract_last = (((1,), (1,)), ((), ()))
    gate_out = lax.dot_general(
        slot_rows, gate_weight, contract_last, preferred_element_type=jnp.float32
    )
    up_out = lax.dot_general(
        slot_rows, up_weight, contract_last, preferred_element_type=jnp.float32
    )
    hidden = (jax.nn.silu(gate_out) * up_out).astype(jnp.bfloat16)
    return jnp.dot(hidden, down_weight, preferred_element_type=jnp.float32).astype(jnp.bfloat16)


def weigh_choices(shares, picked):
    choice_total = picked.shape[1]
    weighted = shares[:, 0:1] * picked[:, 0]
    for which in range(1, choice_total):
        weighted = weighted + shares[:, which : which + 1] * picked[:, which]
    return weighted


def routed_on_device(tokens, norm_gain, expert_ids, route_weights, w_gate, w_up, w_down):
    ep_size = lax.axis_size("ep")
    rep_size = lax.axis_size("rep")
    step_count = tokens.shape[0]
    row_count = tokens.shape[3]
    model_width = tokens.shape[4]
    choice_count = expert_ids.shape[4]
    local_experts = w_gate.shape[0]
    experts = local_experts * ep_size
    block_rows = rep_size * row_count
    capacity = block_rows * choice_count * 5 // (4 * experts)
    column_width = model_width // rep_size
    assigned = block_rows * choice_count
    row_of = jnp.arange(assigned, dtype=jnp.int32) // choice_count
    outputs = []
    for step_index in range(step_count):
        own_normed = norm_rows(tokens[step_index, 0, 0], norm_gain)
        step_weights = route_weights[step_index].reshape(block_rows, choice_count)
        shares = step_weights / jnp.sum(step_weights, axis=1, keepdims=True)
        chosen_ids = expert_ids[step_index].reshape(assigned)
        target = chosen_ids // local_experts
        slot_index = chosen_ids % local_experts
        buckets = ep_size * local_experts
        bucket = target * local_experts + slot_index
        onehot = (bucket[:, None] == jnp.arange(buckets, dtype=jnp.int32)[None, :]).astype(
            jnp.int32
        )
        position = jnp.sum((jnp.cumsum(onehot, axis=0) - onehot) * onehot, axis=1)
        flat_index = bucket * capacity + position
        source_row = (
            jnp.full((buckets * capacity,), block_rows, jnp.int32).at[flat_index].set(row_of)
        )
        own_part = lax.all_to_all(own_normed, "rep", split_axis=1, concat_axis=0, tiled=True)
        padded = jnp.concatenate([own_part, jnp.zeros((1, column_width), jnp.bfloat16)], axis=0)
        outgoing = jnp.take(padded, source_row, axis=0).reshape(
            ep_size, local_experts, capacity, column_width
        )
        received = lax.all_to_all(outgoing, "ep", split_axis=0, concat_axis=0, tiled=True)
        arrived = lax.all_gather(received, "rep", axis=3, tiled=True)
        slot_results = []
        for local_slot in range(local_experts):
            weights_now = (w_gate[local_slot], w_up[local_slot], w_down[local_slot])
            slot_rows = arrived[:, local_slot].reshape(ep_size * capacity, model_width)
            slot_out = expert_partial(slot_rows, weights_now[0], weights_now[1], weights_now[2])
            slot_results.append(slot_out.reshape(ep_size, capacity, model_width))
        results_out = jnp.stack(slot_results, axis=1)
        summed = lax.psum_scatter(
            results_out.astype(jnp.float32).astype(jnp.bfloat16),
            "rep",
            scatter_dimension=3,
            tiled=True,
        ).astype(jnp.float32)
        back = lax.all_to_all(
            summed.astype(jnp.bfloat16), "ep", split_axis=0, concat_axis=0, tiled=True
        ).astype(summed.dtype)
        picked = jnp.take(back.reshape(buckets * capacity, column_width), flat_index, axis=0)
        picked = picked.reshape(block_rows, choice_count, column_width)
        weighted = weigh_choices(shares, picked)
        mixed = (
            lax.all_to_all(
                weighted.astype(jnp.bfloat16), "rep", split_axis=0, concat_axis=1, tiled=True
            )
            .astype(weighted.dtype)
            .astype(jnp.bfloat16)
        )
        outputs.append(mixed)
    return jnp.stack(outputs)[:, None, None]


LANES = 128
HALF = LANES // 2
CHUNKS = 4


def fused_kernel(
    tok_ref, gain_ref, ids_ref, rw_ref, gate_hbm, up_hbm, down_hbm, out_ref,
    wgu, wdn, xg, wx, xs, acc, hs, nrm, wst,
    pbuf, rb0, sb1, rb1, sb2, rb2, sb3, sv, rb3, ost,
    wsem, ag_send, ag_recv, rs_send, rs_recv,
):
    f32, bf16 = jnp.float32, jnp.bfloat16
    steps, rows, width = tok_ref.shape
    nz = xg.shape[4]
    cw = xg.shape[6]
    own_rows = steps * rows
    local_experts, hidden_units = gate_hbm.shape[0], gate_hbm.shape[1]
    choices = ids_ref.shape[3]
    total = 8 * nz * own_rows
    rep, ep = lax.axis_index("rep"), lax.axis_index("ep")
    y, x = rep // 2, rep % 2
    z, core = ep // 2, ep % 2
    partner = (rep, z * 2 + 1 - core)
    over_x = (y * 2 + 1 - x, ep)
    over_y = ((1 - y) * 2 + x, ep)
    along_z = [(rep, ((z + d) % nz) * 2 + core) for d in range(1, nz)]

    barrier = pltpu.get_barrier_semaphore()
    everyone = [partner, over_x, over_y] + along_z
    for device in everyone:
        pl.semaphore_signal(barrier, inc=1, device_id=device, device_id_type=pl.DeviceIdType.MESH)

    loads = []
    for j in range(local_experts):
        loads.append(pltpu.make_async_copy(gate_hbm.at[j], wgu.at[j], wsem.at[len(loads)]))
        loads.append(pltpu.make_async_copy(up_hbm.at[j], wgu.at[local_experts + j], wsem.at[len(loads)]))
    downs = []
    for j in range(local_experts):
        downs.append(
            pltpu.make_async_copy(
                down_hbm.at[j],
                wdn.at[pl.ds(j * hidden_units, hidden_units)],
                wsem.at[len(loads) + j],
            )
        )
    for load in loads + downs:
        load.start()

    for s in range(steps):
        nrm[pl.ds(s * rows, rows), :] = tok_ref[s].astype(f32)
    values = nrm[...]
    scaled = lax.rsqrt(jnp.mean(values * values, axis=-1, keepdims=True) + epsilon)
    for c in range(CHUNKS):
        cols = pl.ds(c * cw, cw)
        xg[c, core, y, x, z] = (nrm[:, cols] * scaled * gain_ref[:, cols]).astype(bf16)
    pl.semaphore_wait(barrier, len(everyone))

    started = []

    def send(src, dst, send_sem, recv_sem, device):
        copy = pltpu.make_async_remote_copy(
            src_ref=src, dst_ref=dst, send_sem=send_sem, recv_sem=recv_sem,
            device_id=device, device_id_type=pl.DeviceIdType.MESH,
        )
        copy.start()
        started.append(copy)
        return copy

    bufs = [xg.at[c] for c in range(CHUNKS)] + [wx]
    order = list(range(CHUNKS)) + [CHUNKS]
    x_first = [(c + 1) % 4 < 2 for c in range(CHUNKS)] + [False]
    first_device = [over_x if flag else over_y for flag in x_first]
    second_device = [over_y if flag else over_x for flag in x_first]

    hop_z, hop_1, hop_2, share_1, share_2, share_3 = {}, {}, {}, {}, {}, {}

    def ag_send_to(c, slot, where, device):
        ref = bufs[c].at[where]
        return send(ref, ref, ag_send.at[c, slot], ag_recv.at[c, slot], device)

    def hop_along_z(c):
        hop_z[c] = [ag_send_to(c, d, (core, y, x, z), along_z[d]) for d in range(nz - 1)]
        hop_1[c] = [ag_send_to(c, nz - 1, (core, y, x, z), first_device[c])]

    for c in order[:-1]:
        hop_along_z(c)
    lane = lax.broadcasted_iota(jnp.int32, (rows, LANES), 1)
    for s in range(steps):
        weights_now = rw_ref[s, rep]
        ids_now = ids_ref[s, rep]
        shares = weights_now / jnp.sum(weights_now, axis=1, keepdims=True)
        dense = jnp.zeros((rows, LANES), f32)
        for k in range(choices):
            dense = dense + jnp.where((lane & (HALF - 1)) == ids_now[:, k : k + 1], shares[:, k : k + 1], 0.0)
        wst[pl.ds(s * rows, rows), :] = dense
    dense = wst[...]
    high = dense.astype(bf16).astype(f32)
    wide_lane = lax.broadcasted_iota(jnp.int32, (own_rows, LANES), 1)
    wx[core, y, x, z] = jnp.where(wide_lane < HALF, high, dense - high).astype(bf16)
    hop_along_z(CHUNKS)
    for c in order:
        for d, copy in enumerate(hop_z[c]):
            copy.wait_recv()
            came_from = (core, y, x, (z - d - 1 + nz) % nz)
            hop_1[c].append(ag_send_to(c, nz + d, came_from, first_device[c]))
        share_1[c] = ag_send_to(c, 2 * nz, (core, y, x), partner)
    for c in order:
        for copy in hop_1[c]:
            copy.wait_recv()
        if x_first[c]:
            hop_2[c] = ag_send_to(c, 2 * nz - 1, (core, y), second_device[c])
            share_2[c] = ag_send_to(c, 2 * nz + 1, (core, y, 1 - x), partner)
        else:
            hop_2[c] = ag_send_to(c, 2 * nz - 1, (core, slice(None), x), second_device[c])
            share_2[c] = ag_send_to(c, 2 * nz + 1, (core, 1 - y, x), partner)

    def finish_gather(c):
        hop_2[c].wait_recv()
        where = (core, 1 - y) if x_first[c] else (core, slice(None), 1 - x)
        share_3[c] = ag_send_to(c, 2 * nz + 2, where, partner)

    def arrived(c):
        for copy in (share_1[c], share_2[c], share_3[c]):
            copy.wait_recv()

    def gate_up(c):
        arrived(c)
        xs[...] = xg[c].astype(f32).reshape(total, cw).astype(bf16).T
        if c == 0:
            for load in loads:
                load.wait()

        def one(i, carry):
            part = jnp.dot(wgu[i, :, pl.ds(c * cw, cw)], xs[...], preferred_element_type=f32)
            acc[i] = part if c == 0 else acc[i] + part
            return carry

        lax.fori_loop(0, 2 * local_experts, one, 0)

    for at, c in enumerate(order):
        finish_gather(c)
        if at >= 1:
            gate_up(order[at - 1])
    arrived(CHUNKS)

    row_weights = wx[...].astype(f32).reshape(total, LANES).T
    all_lane = lax.broadcasted_iota(jnp.int32, (LANES, total), 0) & (HALF - 1)
    for j in range(local_experts):
        mine = jnp.sum(
            jnp.where(all_lane == ep * local_experts + j, row_weights, 0.0), axis=0, keepdims=True
        )
        gate_out, up_out = acc[j], acc[local_experts + j]
        hs[:, pl.ds(j * hidden_units, hidden_units)] = (
            jax.nn.silu(gate_out) * up_out * mine
        ).T.astype(bf16)
    for load in downs:
        load.wait()

    to_core, to_first, to_second, to_z = {}, {}, {}, {}

    def rs_send_to(c, slot, src, dst, device):
        return send(src, dst, rs_send.at[c, slot], rs_recv.at[c, slot], device)

    def place(c, first, second):
        return (second, first) if x_first[c] else (first, second)

    me_first = [x if x_first[c] else y for c in range(CHUNKS)]
    me_second = [y if x_first[c] else x for c in range(CHUNKS)]

    def pair_sum(c, first, second):
        where = place(c, first, second)
        return pbuf[(c, core) + where].astype(f32) + rb0[(c,) + where].astype(f32)

    def down(c):
        half = cw // 2
        for piece in range(2):
            part = jnp.dot(
                hs[...], wdn[:, pl.ds(c * cw + piece * half, half)], preferred_element_type=f32
            )
            pbuf[c, :, :, :, :, :, pl.ds(piece * half, half)] = part.reshape(
                2, 2, 2, nz, own_rows, half
            ).astype(bf16)
        to_core[c] = rs_send_to(c, nz - 1, pbuf.at[c, 1 - core], rb0.at[c], partner)

    def stage_1(c):
        to_core[c].wait_recv()
        for second in range(2):
            sb1[c, second] = pair_sum(c, 1 - me_first[c], second).astype(bf16)
        to_first[c] = rs_send_to(c, nz, sb1.at[c], rb1.at[c], first_device[c])

    def stage_2(c):
        to_first[c].wait_recv()
        other = 1 - me_second[c]
        sb2[c] = (pair_sum(c, me_first[c], other) + rb1[c, other].astype(f32)).astype(bf16)
        to_second[c] = rs_send_to(c, nz + 1, sb2.at[c], rb2.at[c], second_device[c])

    def stage_3(c):
        to_second[c].wait_recv()
        mine = pair_sum(c, me_first[c], me_second[c]) + rb1[c, me_second[c]].astype(f32) + rb2[c].astype(f32)
        sv[c] = mine
        sb3[c] = mine.astype(bf16)
        to_z[c] = [
            rs_send_to(c, d, sb3.at[c, (z + d + 1) % nz], rb3.at[c, d], along_z[d])
            for d in range(nz - 1)
        ]

    def finish(c):
        whole = sv[c, z]
        for d in range(nz - 1):
            to_z[c][d].wait_recv()
            whole = whole + rb3[c, d].astype(f32)
        ost[:, pl.ds(c * cw, cw)] = whole

    for c in range(CHUNKS):
        down(c)
        if c >= 1:
            stage_1(c - 1)
    stage_1(CHUNKS - 1)
    for c in range(CHUNKS):
        stage_2(c)
    for c in range(CHUNKS):
        stage_3(c)
    for c in range(CHUNKS):
        finish(c)
    for s in range(steps):
        out_ref[s] = ost[pl.ds(s * rows, rows), :]
    for copy in started:
        copy.wait_send()


def fused_on_device(tokens, norm_gain, expert_ids, route_weights, w_gate, w_up, w_down):
    steps, rows, width = tokens.shape[0], tokens.shape[3], tokens.shape[4]
    nz = lax.axis_size("ep") // 2
    local_experts, hidden_units = w_gate.shape[0], w_gate.shape[1]
    own_rows = steps * rows
    cw = width // CHUNKS
    total = 8 * nz * own_rows
    f32, bf16 = jnp.float32, jnp.bfloat16
    vmem = pl.BlockSpec(memory_space=pltpu.VMEM)
    hbm = pl.BlockSpec(memory_space=pl.ANY)
    grid_rows = (nz, own_rows, cw)
    out = pl.pallas_call(
        fused_kernel,
        out_shape=jax.ShapeDtypeStruct((steps, rows, width), f32),
        in_specs=[vmem] * 4 + [hbm] * 3,
        out_specs=vmem,
        scratch_shapes=[
            pltpu.VMEM((2 * local_experts, hidden_units, width), bf16),
            pltpu.VMEM((local_experts * hidden_units, width), bf16),
            pltpu.VMEM((CHUNKS, 2, 2, 2) + grid_rows, bf16),
            pltpu.VMEM((2, 2, 2, nz, own_rows, LANES), bf16),
            pltpu.VMEM((cw, total), bf16),
            pltpu.VMEM((2 * local_experts, hidden_units, total), f32),
            pltpu.VMEM((total, local_experts * hidden_units), bf16),
            pltpu.VMEM((own_rows, width), f32),
            pltpu.VMEM((own_rows, LANES), f32),
            pltpu.VMEM((CHUNKS, 2, 2, 2) + grid_rows, bf16),
            pltpu.VMEM((CHUNKS, 2, 2) + grid_rows, bf16),
            pltpu.VMEM((CHUNKS, 2) + grid_rows, bf16),
            pltpu.VMEM((CHUNKS, 2) + grid_rows, bf16),
            pltpu.VMEM((CHUNKS,) + grid_rows, bf16),
            pltpu.VMEM((CHUNKS,) + grid_rows, bf16),
            pltpu.VMEM((CHUNKS,) + grid_rows, bf16),
            pltpu.VMEM((CHUNKS,) + grid_rows, f32),
            pltpu.VMEM((CHUNKS, nz - 1, own_rows, cw), bf16),
            pltpu.VMEM((own_rows, width), f32),
            pltpu.SemaphoreType.DMA((3 * local_experts,)),
            pltpu.SemaphoreType.DMA((CHUNKS + 1, 2 * nz + 3)),
            pltpu.SemaphoreType.DMA((CHUNKS + 1, 2 * nz + 3)),
            pltpu.SemaphoreType.DMA((CHUNKS, nz + 2)),
            pltpu.SemaphoreType.DMA((CHUNKS, nz + 2)),
        ],
        compiler_params=pltpu.CompilerParams(
            collective_id=0, has_side_effects=True, vmem_limit_bytes=60 * 1024 * 1024
        ),
    )(
        tokens[:, 0, 0],
        norm_gain[None, :],
        expert_ids[:, 0],
        route_weights[:, 0],
        w_gate,
        w_up,
        w_down,
    )
    return out.astype(bf16)[:, None, None]


def on_device(tokens, norm_gain, expert_ids, route_weights, w_gate, w_up, w_down):
    ep_size, rep_size = lax.axis_size("ep"), lax.axis_size("rep")
    own_rows = tokens.shape[0] * tokens.shape[3]
    experts = w_gate.shape[0] * ep_size
    dense = (
        rep_size == 4
        and ep_size % 2 == 0
        and own_rows == 8
        and experts <= min(HALF, 4 * expert_ids.shape[4])
        and own_rows * rep_size * ep_size <= 512
        and tokens.shape[4] % (2 * CHUNKS * LANES) == 0
        and w_gate.shape[1] % LANES == 0
    )
    run = fused_on_device if dense else routed_on_device
    return run(tokens, norm_gain, expert_ids, route_weights, w_gate, w_up, w_down)


def solution(mesh):
    return jax.shard_map(
        on_device,
        mesh=mesh,
        in_specs=(
            P(None, "ep", "rep", None, None),
            P(),
            P(None, "ep", None, None, None),
            P(None, "ep", None, None, None),
            P("ep", "rep", None),
            P("ep", "rep", None),
            P("ep", "rep", None),
        ),
        out_specs=P(None, "ep", "rep", None, None),
        check_vma=False,
    )
```
